256 devices in a mesh: row: 16 (over z_hi, x, core), col: 16 (over y, z_lo).
Axes of the slice: x: 4, y: 4, z: 8 (z_hi: 2, z_lo: 4; z = z_hi * 4 + z_lo), core: 2. Of those that a mesh axis runs over, the one named last changes fastest.
Arguments:
- start_block: float32 [65536, 128], P(('row', 'col')), may hold values from -6 to 6
- block_values: float32 [16, 32, 512, 512], P('row', 'col'), may hold values from -0.125 to 0.125
- block_rows: int32 [16, 32], P('row', 'col'), may hold values from 0 to 7, as said below
- block_cols: int32 [16, 32], P('row', 'col'), may hold values from 0 to 7
- block_count: int32 [16, 16], P('row', 'col'), may hold values from 1 to 2, as said below
- center: float32 [1], replicated, may hold values from 0.5 to 1
- radius: float32 [1], replicated, may hold values from 0.8 to 1.2
Outputs:
- basis_block: float32 [65536, 128], P(('row', 'col'))
- projected: float32 [128, 128], replicated
The draws below stay inside these ranges and needn't reach their ends.
Inputs may be any that keep to these rules, and one draw needn't show every extreme that they name: `block_rows`: block row within the tile; the used slots of one tile name distinct block positions. `block_count`: some tile holds exactly 2 used slots in every draw.
All inputs are finite; a program needn't handle non-finite values.
Results may differ from the reference program's by a relative error of at most 0.0003.
Values sent between devices are 32-bit elements; how exact they have to be, the bound alone decides.
A program may use at most 64 MiB of HBM per device.

```python
import jax
import jax.numpy as jnp
from jax import lax

ORDER = 65536
BS = 512
VEC = 128
NB = 2
FILTER_DEG = 2
TILE_ROWS = 8
TILE_COLS = 8
N_ROW = 16
N_COL = 16


def tile_positions(key):
    cell_total = TILE_ROWS * TILE_COLS
    scores = jax.random.randint(key, (N_ROW * N_COL, cell_total), 0, 1 << 20)
    scores = scores * cell_total + jnp.arange(cell_total, dtype=jnp.int32)[None, :]
    chosen = jnp.argsort(scores, axis=-1, stable=True)[:, :NB].astype(jnp.int32)
    return chosen.reshape(N_ROW, N_COL * NB)


def draw_block_rows(key, part):
    return (tile_positions(jax.random.fold_in(key, 7)) // TILE_COLS).astype(jnp.int32)


def draw_block_cols(key, part):
    return (tile_positions(jax.random.fold_in(key, 7)) % TILE_COLS).astype(jnp.int32)


def draw_block_count(key, part):
    key_list = jax.random.split(jax.random.fold_in(key, 13), 3)
    first_draw = jax.random.randint(key_list[0], (N_ROW * N_COL,), 0, NB)
    second_draw = jax.random.randint(key_list[1], (N_ROW * N_COL,), 0, NB)
    counts = jnp.minimum(first_draw, second_draw) + 1
    busiest = jax.random.randint(key_list[2], (), 0, N_ROW * N_COL)
    counts = jnp.where(jnp.arange(N_ROW * N_COL) == busiest, NB, counts)
    return counts.reshape(N_ROW, N_COL).astype(jnp.int32)


def levels(own_key, dims, cuts, low, top_value):
    gain, own = 1.0, jax.random.fold_in(own_key, 6)
    for position, parts in cuts:
        draws = jnp.exp(jax.random.uniform(jax.random.fold_in(own, position), (parts,), jnp.float32, low / len(cuts), top_value / len(cuts)))
        gain = gain * jnp.repeat(draws, dims[position] // parts).reshape([-1 if axis == position else 1 for axis in range(len(dims))])
    return gain


def scatter_about(key, dims, spread, limit, cuts=(), held_as=jnp.bfloat16):
    drawn = jax.random.normal(key, dims, jnp.float32) * spread
    if len(cuts) > 0:
        drawn = levels(key, dims, cuts, -0.22, 0.18) * drawn
    return jnp.clip(drawn, min=-limit, max=limit).astype(held_as)


def setup_inputs(seed: int = 0) -> dict:
    key_of = jax.random.split(jax.random.key(seed), 8)
    start_block = scatter_about(key_of[0], (ORDER, VEC), 1.0, 6.0, ((0, 256),), jnp.float32)
    block_values = scatter_about(key_of[1], (N_ROW, N_COL * NB, BS, BS), (BS * max(1, NB * N_COL // TILE_ROWS)) ** -0.5, 0.125, ((0, 16), (1, 16)), jnp.float32)
    block_rows = draw_block_rows(jax.random.fold_in(key_of[7], 71), 0)
    block_cols = draw_block_cols(jax.random.fold_in(key_of[7], 71), 0)
    block_count = draw_block_count(jax.random.fold_in(key_of[7], 71), 0)
    center = jnp.clip(jax.random.uniform(key_of[5], (1,), jnp.float32, 0.5, 1.0), 0.5, 1.0)
    radius = jnp.clip(jax.random.uniform(key_of[6], (1,), jnp.float32, 0.8, 1.2), 0.8, 1.2)
    return {"start_block": start_block, "block_values": block_values, "block_rows": block_rows, "block_cols": block_cols, "block_count": block_count, "center": center, "radius": radius}


HIGHEST_PRECISION = lax.Precision.HIGHEST

def half_product(vectors, block_values, block_rows, block_cols, block_count, transpose):
    vec_blocks = vectors.reshape(ORDER // BS, BS, VEC)
    slot_rank = jnp.arange(N_COL * NB, dtype=jnp.int32)
    group_ids = (slot_rank // NB).astype(jnp.int32)
    slot_within = (slot_rank % NB).astype(jnp.int32)

    def per_row(running, inputs):
        values, rows_here, cols_here, counts_here, row_group = inputs
        row_ids = (row_group * TILE_ROWS + rows_here).astype(jnp.int32)
        col_ids = (group_ids * TILE_COLS + cols_here).astype(jnp.int32)
        live_mask = (slot_within < counts_here[group_ids]).astype(jnp.float32)
        if transpose:
            picked = vec_blocks[row_ids]
            products = jnp.einsum('sba,sbv->sav', values, picked, precision=HIGHEST_PRECISION)
            products = products * live_mask[:, None, None]
            running = running + jax.ops.segment_sum(products, col_ids, ORDER // BS)
        else:
            picked = vec_blocks[col_ids]
            products = jnp.einsum('sab,sbv->sav', values, picked, precision=HIGHEST_PRECISION)
            products = products * live_mask[:, None, None]
            running = running + jax.ops.segment_sum(products, row_ids, ORDER // BS)
        return (running, None)
    zeros_start = jnp.zeros((ORDER // BS, BS, VEC), jnp.float32)
    inputs = (block_values, block_rows, block_cols, block_count, jnp.arange(N_ROW, dtype=jnp.int32))
    running, unused = lax.scan(per_row, zeros_start, inputs)
    return running.reshape(ORDER, VEC)

def reference(start_block, block_values, block_rows, block_cols, block_count, center, radius):

    def apply_scaled(vectors):
        middle = half_product(vectors, block_values, block_rows, block_cols, block_count, True)
        system = half_product(middle, block_values, block_rows, block_cols, block_count, False)
        return (system - center[0] * vectors) / radius[0]
    previous = start_block
    current = apply_scaled(start_block)
    for degree_step in range(FILTER_DEG - 1):
        following = 2.0 * apply_scaled(current) - previous
        previous = current
        current = following
    gram_matrix = jnp.dot(current.T, current, precision=HIGHEST_PRECISION)
    lower_factor = jnp.linalg.cholesky(gram_matrix)
    basis_block = jax.scipy.linalg.solve_triangular(lower_factor, current.T, lower=True).T
    image_block = half_product(basis_block, block_values, block_rows, block_cols, block_count, True)
    projected = jnp.dot(image_block.T, image_block, precision=HIGHEST_PRECISION)
    return (basis_block, projected)
```

```python
import functools

import jax
import jax.numpy as jnp
from jax import lax
from jax.experimental import pallas as pl
from jax.experimental.pallas import tpu as pltpu
from jax.sharding import PartitionSpec as P

BS = 512
VEC = 128
R = 256
HIGHEST = lax.Precision.HIGHEST
MESH = pl.DeviceIdType.MESH
F32 = jnp.float32


def wrap(value, by, n):
    return lax.rem(value + (by + n), n)


class Place:
    def __init__(self):
        self.row, self.col = lax.axis_index("row"), lax.axis_index("col")
        self.core = lax.rem(self.row, 2)
        self.x = lax.rem(lax.div(self.row, 2), 4)
        self.zh = lax.div(self.row, 8)
        self.z = lax.rem(self.col, 4)
        self.y = lax.div(self.col, 4)

    def at(self, core=None, x=None, zh=None, y=None, z=None):
        core = self.core if core is None else core
        x = self.x if x is None else x
        zh = self.zh if zh is None else zh
        y = self.y if y is None else y
        z = self.z if z is None else z
        return (zh * 8 + x * 2 + core, y * 4 + z)

    def other_core(self):
        return self.at(core=1 - self.core)

    def other_half(self):
        return self.at(zh=1 - self.zh)

    def x_by(self, d):
        return self.at(x=wrap(self.x, d, 4))

    def y_by(self, d):
        return self.at(y=wrap(self.y, d, 4))

    def z_by(self, d):
        return self.at(z=wrap(self.z, d, 4))


class Wire:
    def __init__(self, send_sem, recv_sem):
        self.send_sem, self.recv_sem, self.open = send_sem, recv_sem, []

    def copy(self, src, dst, i, device):
        return pltpu.make_async_remote_copy(
            src_ref=src, dst_ref=dst, send_sem=self.send_sem.at[i], recv_sem=self.recv_sem.at[i],
            device_id=device, device_id_type=MESH)

    def send(self, src, dst, i, device):
        one = self.copy(src, dst, i, device)
        one.start()
        self.open.append(one)

    def recv(self, dst, i, device):
        self.copy(dst, dst, i, device).wait_recv()

    def drain(self):
        for one in self.open:
            one.wait_send()
        self.open = []


def greet(devices):
    barrier = pltpu.get_barrier_semaphore()
    for device in devices:
        pl.semaphore_signal(barrier, inc=1, device_id=device, device_id_type=MESH)
    pl.semaphore_wait(barrier, len(devices))


def col_peers(me):
    return [me.y_by(1), me.y_by(-1), me.z_by(1), me.z_by(2), me.z_by(3)]


def row_peers(me):
    return [me.other_core(), me.x_by(1), me.x_by(-1), me.other_half()]


AG_COL = 19


def col_gather(me, wire, g, base):
    h = R // 2
    yp, ym, y2 = wrap(me.y, 1, 4), wrap(me.y, -1, 4), wrap(me.y, 2, 4)
    up, down = me.y_by(1), me.y_by(-1)
    zs = [wrap(me.z, -k, 4) for k in range(4)]
    for k in (1, 3, 2):
        wire.send(g.at[me.col], g.at[me.col], base + k - 1, me.z_by(k))

    def full(k):
        s = me.y * 4 + zs[k]
        wire.send(g.at[s], g.at[s], base + 3 + k, up)
        wire.send(g.at[s], g.at[s], base + 7 + k, down)

    def forward(k):
        s = ym * 4 + zs[k]
        wire.recv(g.at[s], base + 3 + k, down)
        wire.send(g.at[s, 0:h], g.at[s, 0:h], base + 11 + k, up)
        s = yp * 4 + zs[k]
        wire.recv(g.at[s], base + 7 + k, up)
        wire.send(g.at[s, h:R], g.at[s, h:R], base + 15 + k, down)

    full(0)
    last = 0
    for k in (1, 3, 2):
        wire.recv(g.at[me.y * 4 + zs[k]], base + k - 1, me.z_by(-k))
        full(k)
        forward(last)
        last = k
    forward(last)
    for k in (0, 1, 3, 2):
        s = y2 * 4 + zs[k]
        wire.recv(g.at[s, 0:h], base + 11 + k, down)
        wire.recv(g.at[s, h:R], base + 15 + k, up)


RS_COL = 27


def col_scatter(me, wire, p, far, near, side, base):
    h = R // 2
    yp, ym, y2 = wrap(me.y, 1, 4), wrap(me.y, -1, 4), wrap(me.y, 2, 4)
    up, down = me.y_by(1), me.y_by(-1)
    zs = [wrap(me.z, k, 4) for k in range(4)]

    def start(k):
        s = y2 * 4 + zs[k]
        wire.send(p.at[s, 0:h], far.at[0, k], base + k, up)
        wire.send(p.at[s, h:R], far.at[1, k], base + 4 + k, down)

    def direct(k):
        s = yp * 4 + zs[k]
        wire.send(p.at[s, h:R], near.at[0, k, h:R], base + 8 + k, up)
        s = ym * 4 + zs[k]
        wire.send(p.at[s, 0:h], near.at[1, k, 0:h], base + 12 + k, down)

    def relay(k):
        s = yp * 4 + zs[k]
        wire.recv(far.at[0, k], base + k, down)
        far[0, k] = far[0, k] + p[s, 0:h]
        wire.send(far.at[0, k], near.at[0, k, 0:h], base + 16 + k, up)
        s = ym * 4 + zs[k]
        wire.recv(far.at[1, k], base + 4 + k, up)
        far[1, k] = far[1, k] + p[s, h:R]
        wire.send(far.at[1, k], near.at[1, k, h:R], base + 20 + k, down)

    def finish(k):
        s = me.y * 4 + zs[k]
        wire.recv(near.at[0, k, h:R], base + 8 + k, down)
        wire.recv(near.at[0, k, 0:h], base + 16 + k, down)
        wire.recv(near.at[1, k, 0:h], base + 12 + k, up)
        wire.recv(near.at[1, k, h:R], base + 20 + k, up)
        total = p[s] + near[0, k] + near[1, k]
        if k == 0:
            return total
        near[0, k] = total
        wire.send(near.at[0, k], side.at[k - 1], base + 23 + k, me.z_by(k))

    order = (2, 1, 3, 0)
    start(2)
    start(1)
    direct(2)
    relay(2)
    start(3)
    direct(1)
    relay(1)
    finish(2)
    start(0)
    direct(3)
    relay(3)
    finish(1)
    direct(0)
    relay(0)
    finish(3)
    total = finish(0)
    for k in order[:3]:
        wire.recv(side.at[k - 1], base + 23 + k, me.z_by(-k))
        total = total + side[k - 1]
    return total


RS_ROW = 11


def row_scatter(me, wire, p, pair, far, near, side, base):
    xp, xm, x2 = wrap(me.x, 1, 4), wrap(me.x, -1, 4), wrap(me.x, 2, 4)
    up, down, mate = me.x_by(1), me.x_by(-1), me.other_core()
    to = [me.x, xp, x2, xm]
    for k in (2, 1, 3, 0):
        wire.send(p.at[:, to[k], 1 - me.core], pair.at[k], base + k, mate)

    def join(k):
        wire.recv(pair.at[k], base + k, mate)
        pair[k] = pair[k] + p[:, to[k], me.core]

    join(2)
    wire.send(pair.at[2, 0], far.at[0], base + 4, up)
    wire.send(pair.at[2, 1], far.at[1], base + 5, down)
    join(1)
    wire.send(pair.at[1, 1], near.at[0, 1], base + 6, up)
    join(3)
    wire.send(pair.at[3, 0], near.at[1, 0], base + 7, down)
    join(0)
    wire.recv(far.at[0], base + 4, down)
    far[0] = far[0] + pair[1, 0]
    wire.send(far.at[0], near.at[0, 0], base + 8, up)
    wire.recv(far.at[1], base + 5, up)
    far[1] = far[1] + pair[3, 1]
    wire.send(far.at[1], near.at[1, 1], base + 9, down)
    wire.recv(near.at[0, 1], base + 6, down)
    wire.recv(near.at[1, 0], base + 7, up)
    wire.recv(near.at[0, 0], base + 8, down)
    wire.recv(near.at[1, 1], base + 9, up)
    other = 1 - me.zh
    near[0, other] = near[0, other] + near[1, other] + pair[0, other]
    wire.send(near.at[0, other], side, base + 10, me.other_half())
    total = near[0, me.zh] + near[1, me.zh] + pair[0, me.zh]
    wire.recv(side, base + 10, me.other_half())
    return total + side[...]


AG_ROW = 17


def row_gather(me, wire, g, base):
    h = R // 2
    xp, xm, x2 = wrap(me.x, 1, 4), wrap(me.x, -1, 4), wrap(me.x, 2, 4)
    up, down, mate = me.x_by(1), me.x_by(-1), me.other_core()
    half = [me.zh, 1 - me.zh]
    mine = g.at[me.zh, me.x, me.core]
    wire.send(mine, mine, base, me.other_half())

    def full(k):
        one = g.at[half[k], me.x, me.core]
        wire.send(one, one, base + 1 + k, up)
        wire.send(one, one, base + 3 + k, down)
        wire.send(one, one, base + 9 + k, mate)

    def forward(k):
        one = g.at[half[k], xm, me.core]
        wire.recv(one, base + 1 + k, down)
        part = g.at[half[k], xm, me.core, 0:h]
        wire.send(part, part, base + 5 + k, up)
        wire.send(one, one, base + 11 + k, mate)
        one = g.at[half[k], xp, me.core]
        wire.recv(one, base + 3 + k, up)
        part = g.at[half[k], xp, me.core, h:R]
        wire.send(part, part, base + 7 + k, down)
        wire.send(one, one, base + 13 + k, mate)

    def far(k):
        wire.recv(g.at[half[k], x2, me.core, 0:h], base + 5 + k, down)
        wire.recv(g.at[half[k], x2, me.core, h:R], base + 7 + k, up)
        one = g.at[half[k], x2, me.core]
        wire.send(one, one, base + 15 + k, mate)

    full(0)
    forward(0)
    wire.recv(g.at[half[1], me.x, me.core], base, me.other_half())
    full(1)
    far(0)
    forward(1)
    far(1)
    for first, where in ((9, me.x), (11, xm), (13, xp), (15, x2)):
        for k in range(2):
            wire.recv(g.at[half[k], where, 1 - me.core], base + first + k, mate)


def gather_kernel(v_ref, g_ref, send_sem, recv_sem, own_sem):
    me, wire = Place(), Wire(send_sem, recv_sem)
    own = pltpu.make_async_copy(v_ref, g_ref.at[me.col], own_sem)
    own.start()
    greet(col_peers(me))
    own.wait()
    col_gather(me, wire, g_ref, 0)
    wire.drain()


def row_sum_kernel(p_ref, g_ref, pair, far, near, side, send_sem, recv_sem):
    me, wire = Place(), Wire(send_sem, recv_sem)
    greet(row_peers(me))
    g_ref[me.zh, me.x, me.core] = row_scatter(me, wire, p_ref, pair, far, near, side, 0)
    row_gather(me, wire, g_ref, RS_ROW)
    wire.drain()


def row_scatter_kernel(p_ref, z_ref, pair, far, near, side, send_sem, recv_sem):
    me, wire = Place(), Wire(send_sem, recv_sem)
    greet(row_peers(me))
    z_ref[...] = row_scatter(me, wire, p_ref, pair, far, near, side, 0)
    wire.drain()


def col_sum_kernel(first, center, radius, p_ref, y_ref, old_ref, g_ref, new_ref, far, near, side, send_sem, recv_sem):
    me, wire = Place(), Wire(send_sem, recv_sem)
    greet(col_peers(me))
    system = col_scatter(me, wire, p_ref, far, near, side, 0)
    new = (system - center[0] * y_ref[...]) / radius[0]
    if not first:
        new = 2.0 * new - old_ref[...]
    new_ref[...] = new
    g_ref[me.col] = new
    col_gather(me, wire, g_ref, RS_COL)
    wire.drain()


def sums_kernel(a_ref, o_ref, mine, pair, xs, xsum, ys, zs, send_sem, recv_sem):
    me, wire = Place(), Wire(send_sem, recv_sem)
    mate = me.other_core()
    deep = me.zh * 4 + me.z
    zdev = [me.at(zh=lax.div(wrap(deep, d, 8), 4), z=lax.rem(wrap(deep, d, 8), 4)) for d in range(8)]
    greet([mate] + [me.x_by(d) for d in (1, 2, 3)] + [me.y_by(d) for d in (1, 2, 3)] + zdev[1:])
    wire.send(a_ref.at[1 - me.core], pair, 0, mate)
    wire.recv(pair, 0, mate)
    mine[...] = a_ref[me.core] + pair[...]
    for d in (2, 1, 3):
        wire.send(mine.at[wrap(me.x, d, 4)], xs.at[d - 1], d, me.x_by(d))
    total = mine[me.x]
    for d in (1, 3, 2):
        wire.recv(xs.at[d - 1], d, me.x_by(-d))
        total = total + xs[d - 1]
    xsum[...] = total
    for d in (2, 1, 3):
        wire.send(xsum.at[wrap(me.y, d, 4)], ys.at[d - 1], 3 + d, me.y_by(d))
    total = xsum[me.y]
    for d in (1, 3, 2):
        wire.recv(ys.at[d - 1], 3 + d, me.y_by(-d))
        total = total + ys[d - 1]
    zs[deep] = total
    for d in (4, 3, 5, 2, 6, 1, 7):
        wire.send(zs.at[deep], zs.at[deep], 6 + d, zdev[d])
    for d in (1, 7, 2, 6, 3, 5, 4):
        wire.recv(zs.at[wrap(deep, -d, 8)], 6 + d, zdev[8 - d])
    total = zs[0]
    for d in range(1, 8):
        total = total + zs[d]
    o_ref[me.core, me.x, me.y] = total
    part = o_ref.at[me.core, me.x, me.y]
    for d in (2, 1, 3):
        wire.send(part, part, 13 + d, me.y_by(d))
    for d in (1, 3, 2):
        wire.recv(o_ref.at[me.core, me.x, wrap(me.y, -d, 4)], 13 + d, me.y_by(-d))
    part = o_ref.at[me.core, me.x]
    for d in (2, 1, 3):
        wire.send(part, part, 16 + d, me.x_by(d))
    for d in (1, 3, 2):
        wire.recv(o_ref.at[me.core, wrap(me.x, -d, 4)], 16 + d, me.x_by(-d))
    wire.send(o_ref.at[me.core], o_ref.at[me.core], 20, mate)
    wire.recv(o_ref.at[1 - me.core], 20, mate)
    wire.drain()


def product_kernel(transpose, take, put, count, values, g_ref, p_ref):
    p_ref[...] = jnp.zeros_like(p_ref)
    dims = (((0,), (0,)), ((), ())) if transpose else (((1,), (0,)), ((), ()))
    for s in range(2):
        got = lax.dot_general(values[s], g_ref[jnp.clip(take[s], 0, 7)], dims, precision=HIGHEST, preferred_element_type=F32)
        got = jnp.where(s < count[0], got, 0.0)
        where = jnp.clip(put[s], 0, 7)
        p_ref[where] = p_ref[where] + got


VMEM = pl.BlockSpec(memory_space=pltpu.VMEM)
SMEM = pl.BlockSpec(memory_space=pltpu.SMEM)


def buf(*dims):
    return pltpu.VMEM(dims, F32)


def out(*dims):
    return jax.ShapeDtypeStruct(dims, F32)


def sems(n):
    return [pltpu.SemaphoreType.DMA((n,)), pltpu.SemaphoreType.DMA((n,))]


def remote(kernel, ident, in_specs, outs, scratch):
    many = isinstance(outs, tuple)
    return pl.pallas_call(
        kernel, out_shape=outs, in_specs=in_specs, out_specs=(VMEM,) * len(outs) if many else VMEM, scratch_shapes=scratch,
        compiler_params=pltpu.CompilerParams(collective_id=ident, has_side_effects=True))


def row_scratch():
    return [buf(4, 2, R, VEC), buf(2, R, VEC), buf(2, 2, R, VEC), buf(R, VEC)]


def col_scratch():
    return [buf(2, 4, R // 2, VEC), buf(2, 4, R, VEC), buf(3, R, VEC)]


def gather_col(v, ident):
    return remote(gather_kernel, ident, [VMEM], out(16, R, VEC), sems(AG_COL) + [pltpu.SemaphoreType.DMA])(v)


def sum_row(p, ident):
    return remote(row_sum_kernel, ident, [VMEM], out(2, 4, 2, R, VEC), row_scratch() + sems(RS_ROW + AG_ROW))(p.reshape(2, 4, 2, R, VEC))


def scatter_row(p, ident):
    return remote(row_scatter_kernel, ident, [VMEM], out(R, VEC), row_scratch() + sems(RS_ROW))(p.reshape(2, 4, 2, R, VEC))


def sum_col(p, y, old, center, radius, first, ident):
    return remote(functools.partial(col_sum_kernel, first), ident, [SMEM, SMEM, VMEM, VMEM, VMEM],
                  (out(16, R, VEC), out(R, VEC)), col_scratch() + sems(RS_COL + AG_COL))(center, radius, p.reshape(16, R, VEC), y, old)


def sum_all(a, ident):
    scratch = [buf(4, 4, 8, VEC), buf(4, 4, 8, VEC), buf(3, 4, 8, VEC), buf(4, 8, VEC), buf(3, 8, VEC), buf(8, 8, VEC)]
    return remote(sums_kernel, ident, [VMEM], out(2, 4, 4, 8, VEC), scratch + sems(21))(a.reshape(2, 4, 4, 8, VEC)).reshape(2, VEC, VEC)


def product(transpose, values, take, put, count, g):
    return pl.pallas_call(
        functools.partial(product_kernel, transpose), out_shape=out(8, BS, VEC), in_specs=[SMEM, SMEM, SMEM, VMEM, VMEM], out_specs=VMEM,
    )(take, put, count, values, g.reshape(8, BS, VEC))


def body(start_block, block_values, block_rows, block_cols, block_count, center, radius):
    values, rows, cols, count = block_values[0], block_rows[0], block_cols[0], block_count[0]
    ident = 0
    older, newer = start_block, start_block
    whole = gather_col(start_block, ident)
    for first in (True, False):
        part = product(True, values, rows, cols, count, whole)
        middle = sum_row(part, ident + 1)
        part = product(False, values, cols, rows, count, middle)
        whole, newest = sum_col(part, newer, older, center, radius, first, ident + 2)
        older, newer = newer, newest
        ident += 2
    part = product(True, values, rows, cols, count, whole)
    image = scatter_row(part, ident + 1)
    squares = [jnp.dot(a.T, a, precision=HIGHEST) for a in (newer, image)]
    gram, inner = sum_all(jnp.stack(squares), ident + 2)
    lower = jnp.linalg.cholesky(gram)
    solved = jax.scipy.linalg.solve_triangular(lower, jnp.concatenate([newer.T, inner], axis=1), lower=True)
    basis = solved[:, :R].T
    projected = jax.scipy.linalg.solve_triangular(lower, solved[:, R:].T, lower=True)
    return basis, projected


def solution(mesh):
    in_specs = (P(("row", "col"), None), P("row", "col", None, None), P("row", "col"), P("row", "col"), P("row", "col"), P(), P())
    out_specs = (P(("row", "col"), None), P())
    return jax.shard_map(body, mesh=mesh, in_specs=in_specs, out_specs=out_specs, check_vma=False)
```

```python
import functools

import jax
import jax.numpy as jnp
from jax import lax
from jax.experimental import pallas as pl
from jax.experimental.pallas import tpu as pltpu
from jax.sharding import PartitionSpec as P

BS = 512
VEC = 128
R = 256
STREAMS = 2
W = VEC // STREAMS
LAG = 0
HIGHEST = lax.Precision.HIGHEST
MESH = pl.DeviceIdType.MESH
F32 = jnp.float32


def wrap(value, by, n):
    return lax.rem(value + (by + n), n)


class Place:
    def __init__(self):
        self.row, self.col = lax.axis_index("row"), lax.axis_index("col")
        self.core = lax.rem(self.row, 2)
        self.x = lax.rem(lax.div(self.row, 2), 4)
        self.zh = lax.div(self.row, 8)
        self.z = lax.rem(self.col, 4)
        self.y = lax.div(self.col, 4)

    def at(self, core=None, x=None, zh=None, y=None, z=None):
        core = self.core if core is None else core
        x = self.x if x is None else x
        zh = self.zh if zh is None else zh
        y = self.y if y is None else y
        z = self.z if z is None else z
        return (zh * 8 + x * 2 + core, y * 4 + z)

    def other_core(self):
        return self.at(core=1 - self.core)

    def other_half(self):
        return self.at(zh=1 - self.zh)

    def x_by(self, d):
        return self.at(x=wrap(self.x, d, 4))

    def y_by(self, d):
        return self.at(y=wrap(self.y, d, 4))

    def z_by(self, d):
        return self.at(z=wrap(self.z, d, 4))

    def deep(self):
        deep = self.zh * 4 + self.z
        on = [wrap(deep, d, 8) for d in range(8)]
        return deep, [self.at(zh=lax.div(one, 4), z=lax.rem(one, 4)) for one in on]


class Wire:
    def __init__(self, send_sem, recv_sem):
        self.send_sem, self.recv_sem, self.open = send_sem, recv_sem, []

    def copy(self, src, dst, i, device):
        return pltpu.make_async_remote_copy(
            src_ref=src, dst_ref=dst, send_sem=self.send_sem.at[i], recv_sem=self.recv_sem.at[i],
            device_id=device, device_id_type=MESH)

    def send(self, src, dst, i, device):
        one = self.copy(src, dst, i, device)
        one.start()
        self.open.append(one)

    def recv(self, dst, i, device):
        self.copy(dst, dst, i, device).wait_recv()

    def drain(self):
        for one in self.open:
            one.wait_send()
        self.open = []


def greet(devices):
    barrier = pltpu.get_barrier_semaphore()
    for device in devices:
        pl.semaphore_signal(barrier, inc=1, device_id=device, device_id_type=MESH)
    pl.semaphore_wait(barrier, len(devices))


AG_COL = 19


def col_gather(me, wire, g, base):
    h = W // 2
    yp, ym, y2 = wrap(me.y, 1, 4), wrap(me.y, -1, 4), wrap(me.y, 2, 4)
    up, down = me.y_by(1), me.y_by(-1)
    zs = [wrap(me.z, -k, 4) for k in range(4)]
    for k in (1, 3, 2):
        wire.send(g.at[me.col], g.at[me.col], base + k - 1, me.z_by(k))

    def full(k):
        s = me.y * 4 + zs[k]
        wire.send(g.at[s], g.at[s], base + 3 + k, up)
        wire.send(g.at[s], g.at[s], base + 7 + k, down)

    def forward(k):
        s = ym * 4 + zs[k]
        wire.recv(g.at[s], base + 3 + k, down)
        wire.send(g.at[s, 0:h], g.at[s, 0:h], base + 11 + k, up)
        s = yp * 4 + zs[k]
        wire.recv(g.at[s], base + 7 + k, up)
        wire.send(g.at[s, h:W], g.at[s, h:W], base + 15 + k, down)

    full(0)
    last = 0
    for k in (1, 3, 2):
        yield
        wire.recv(g.at[me.y * 4 + zs[k]], base + k - 1, me.z_by(-k))
        full(k)
        forward(last)
        last = k
    yield
    forward(last)
    yield
    for k in (0, 1, 3, 2):
        s = y2 * 4 + zs[k]
        wire.recv(g.at[s, 0:h], base + 11 + k, down)
        wire.recv(g.at[s, h:W], base + 15 + k, up)


RS_COL = 27


def col_scatter(me, wire, p, far, near, side, total, base):
    h = W // 2
    yp, ym, y2 = wrap(me.y, 1, 4), wrap(me.y, -1, 4), wrap(me.y, 2, 4)
    up, down = me.y_by(1), me.y_by(-1)
    zs = [wrap(me.z, k, 4) for k in range(4)]

    def start(k):
        s = y2 * 4 + zs[k]
        wire.send(p.at[s, 0:h], far.at[0, k], base + k, up)
        wire.send(p.at[s, h:W], far.at[1, k], base + 4 + k, down)

    def direct(k):
        s = yp * 4 + zs[k]
        wire.send(p.at[s, h:W], near.at[0, k, h:W], base + 8 + k, up)
        s = ym * 4 + zs[k]
        wire.send(p.at[s, 0:h], near.at[1, k, 0:h], base + 12 + k, down)

    def relay(k):
        s = yp * 4 + zs[k]
        wire.recv(far.at[0, k], base + k, down)
        far[0, k] = far[0, k] + p[s, 0:h]
        wire.send(far.at[0, k], near.at[0, k, 0:h], base + 16 + k, up)
        s = ym * 4 + zs[k]
        wire.recv(far.at[1, k], base + 4 + k, up)
        far[1, k] = far[1, k] + p[s, h:W]
        wire.send(far.at[1, k], near.at[1, k, h:W], base + 20 + k, down)

    def finish(k):
        s = me.y * 4 + zs[k]
        wire.recv(near.at[0, k, h:W], base + 8 + k, down)
        wire.recv(near.at[0, k, 0:h], base + 16 + k, down)
        wire.recv(near.at[1, k, 0:h], base + 12 + k, up)
        wire.recv(near.at[1, k, h:W], base + 20 + k, up)
        near[0, k] = p[s] + near[0, k] + near[1, k]
        if k > 0:
            wire.send(near.at[0, k], side.at[k - 1], base + 23 + k, me.z_by(k))

    start(2)
    start(1)
    direct(2)
    yield
    relay(2)
    start(3)
    direct(1)
    yield
    relay(1)
    start(0)
    direct(3)
    yield
    finish(2)
    relay(3)
    direct(0)
    yield
    finish(1)
    relay(0)
    yield
    finish(3)
    yield
    finish(0)
    for k in (2, 1, 3):
        wire.recv(side.at[k - 1], base + 23 + k, me.z_by(-k))
    total[...] = near[0, 0] + side[0] + side[1] + side[2]


RS_ROW = 10


def row_scatter(me, wire, p, pair, far, near, base):
    xp, xm, x2 = wrap(me.x, 1, 4), wrap(me.x, -1, 4), wrap(me.x, 2, 4)
    up, down, mate = me.x_by(1), me.x_by(-1), me.other_core()
    to = [me.x, xp, x2, xm]
    for k in (2, 1, 3, 0):
        wire.send(p.at[:, to[k], 1 - me.core], pair.at[k], base + k, mate)

    def join(k):
        wire.recv(pair.at[k], base + k, mate)
        pair[k] = pair[k] + p[:, to[k], me.core]

    yield
    join(2)
    wire.send(pair.at[2, 0], far.at[0], base + 4, up)
    wire.send(pair.at[2, 1], far.at[1], base + 5, down)
    join(1)
    wire.send(pair.at[1, 1], near.at[0, 1], base + 6, up)
    join(3)
    wire.send(pair.at[3, 0], near.at[1, 0], base + 7, down)
    join(0)
    yield
    wire.recv(far.at[0], base + 4, down)
    far[0] = far[0] + pair[1, 0]
    wire.send(far.at[0], near.at[0, 0], base + 8, up)
    wire.recv(far.at[1], base + 5, up)
    far[1] = far[1] + pair[3, 1]
    wire.send(far.at[1], near.at[1, 1], base + 9, down)
    yield
    wire.recv(near.at[0, 1], base + 6, down)
    wire.recv(near.at[1, 0], base + 7, up)
    wire.recv(near.at[0, 0], base + 8, down)
    wire.recv(near.at[1, 1], base + 9, up)
    near[0] = near[0] + near[1] + pair[0]


AG_ROW = 16


def row_gather(me, wire, g, near, side, base):
    xp, xm, x2 = wrap(me.x, 1, 4), wrap(me.x, -1, 4), wrap(me.x, 2, 4)
    up, down, mate = me.x_by(1), me.x_by(-1), me.other_core()
    for k in range(2):
        wire.send(near.at[0, k], side.at[k], base + k, me.other_half())
    yield
    for k in range(2):
        wire.recv(side.at[k], base + k, me.other_half())
        g[k, me.x, me.core] = near[0, k] + side[k]
        one = g.at[k, me.x, me.core]
        first, second = ((up, base + 2), (down, base + 4)) if k == 0 else ((down, base + 4), (up, base + 2))
        wire.send(one, one, first[1] + k, first[0])
        wire.send(one, one, second[1] + k, second[0])
        wire.send(one, one, base + 8 + k, mate)
    yield
    one = g.at[0, xm, me.core]
    wire.recv(one, base + 2, down)
    wire.send(one, one, base + 6, up)
    wire.send(one, one, base + 10, mate)
    one = g.at[1, xp, me.core]
    wire.recv(one, base + 5, up)
    wire.send(one, one, base + 7, down)
    wire.send(one, one, base + 13, mate)
    one = g.at[1, xm, me.core]
    wire.recv(one, base + 3, down)
    wire.send(one, one, base + 11, mate)
    one = g.at[0, xp, me.core]
    wire.recv(one, base + 4, up)
    wire.send(one, one, base + 12, mate)
    yield
    one = g.at[0, x2, me.core]
    wire.recv(one, base + 6, down)
    wire.send(one, one, base + 14, mate)
    one = g.at[1, x2, me.core]
    wire.recv(one, base + 7, up)
    wire.send(one, one, base + 15, mate)
    yield
    for first, where in ((8, me.x), (10, xm), (12, xp), (14, x2)):
        for k in range(2):
            wire.recv(g.at[k, where, 1 - me.core], base + first + k, mate)


def product(transpose, values, take, put, count, load, store):
    dims = (((1,), (0,)), ((), ())) if transpose else (((1,), (1,)), ((), ()))
    got = []
    for s in range(2):
        total = None
        for h in range(2):
            part = values[s, h * R:(h + 1) * R, :] if transpose else values[s, :, h * R:(h + 1) * R]
            one = lax.dot_general(load(take[s], h), part, dims, precision=HIGHEST, preferred_element_type=F32)
            total = one if total is None else total + one
        got.append(total)
    for t in range(8):
        for h in range(2):
            chunk = jnp.where(put[0] == t, got[0][:, h * R:(h + 1) * R], 0.0)
            chunk = chunk + jnp.where(jnp.logical_and(put[1] == t, count[0] > 1), got[1][:, h * R:(h + 1) * R], 0.0)
            store(t, h, chunk)


def stream(me, wire, base, rows, cols, count, center, radius, values, v, new, image, mem):
    mem = iter(mem)

    def get(n):
        return [next(mem) for _ in range(n)]

    def by_row(g):
        return lambda b, h: g[lax.div(b, 4), lax.rem(b, 4), h]

    def by_col(g):
        return lambda b, h: g[2 * b + h]

    (g,) = get(1)
    g[me.col] = v[...]
    yield from col_gather(me, wire, g, base)
    base += AG_COL
    older, newer = v, v
    for first in (True, False):
        p, pair, far, near, side, g_row = get(6)

        def put_row(t, h, chunk):
            p[t // 4, t % 4, h] = chunk

        product(True, values, rows, cols, count, by_col(g), put_row)
        yield from row_scatter(me, wire, p, pair, far, near, base)
        yield from row_gather(me, wire, g_row, near, side, base + RS_ROW)
        base += RS_ROW + AG_ROW
        q, far, near, side, total, g = get(6)

        def put_col(t, h, chunk):
            q[2 * t + h] = chunk

        product(False, values, cols, rows, count, by_row(g_row), put_col)
        yield from col_scatter(me, wire, q, far, near, side, total, base)
        fresh = (total[...] - center[0] * newer[...]) / radius[0]
        if first:
            total[...] = fresh
            older, newer = newer, total
        else:
            fresh = 2.0 * fresh - older[...]
            new[...] = fresh
        g[me.col] = fresh
        yield from col_gather(me, wire, g, base + RS_COL)
        base += RS_COL + AG_COL
    p, pair, far, near, side = get(5)

    def put_last(t, h, chunk):
        p[t // 4, t % 4, h] = chunk

    product(True, values, rows, cols, count, by_col(g), put_last)
    yield from row_scatter(me, wire, p, pair, far, near, base)
    wire.send(near.at[0, 1 - me.zh], side, base + RS_ROW, me.other_half())
    yield
    wire.recv(side, base + RS_ROW, me.other_half())
    image[...] = near[0, me.zh] + side[...]


STREAM_SEMS = AG_COL + 2 * (RS_ROW + AG_ROW + RS_COL + AG_COL) + RS_ROW + 1
SUMS = 21


def sum_all(me, wire, a_ref, o_ref, mine, pair, xs, xsum, ys, zs, base):
    mate = me.other_core()
    deep, zdev = me.deep()
    wire.send(a_ref.at[1 - me.core], pair, base, mate)
    wire.recv(pair, base, mate)
    mine[...] = a_ref[me.core] + pair[...]
    for d in (2, 1, 3):
        wire.send(mine.at[wrap(me.x, d, 4)], xs.at[d - 1], base + d, me.x_by(d))
    for d in (1, 3, 2):
        wire.recv(xs.at[d - 1], base + d, me.x_by(-d))
    xsum[...] = mine[me.x] + xs[0] + xs[1] + xs[2]
    for d in (2, 1, 3):
        wire.send(xsum.at[wrap(me.y, d, 4)], ys.at[d - 1], base + 3 + d, me.y_by(d))
    for d in (1, 3, 2):
        wire.recv(ys.at[d - 1], base + 3 + d, me.y_by(-d))
    zs[deep] = xsum[me.y] + ys[0] + ys[1] + ys[2]
    for d in (4, 3, 5, 2, 6, 1, 7):
        wire.send(zs.at[deep], zs.at[deep], base + 6 + d, zdev[d])
    for d in (1, 7, 2, 6, 3, 5, 4):
        wire.recv(zs.at[wrap(deep, -d, 8)], base + 6 + d, zdev[8 - d])
    total = zs[0]
    for d in range(1, 8):
        total = total + zs[d]
    o_ref[me.core, me.x, me.y] = total
    part = o_ref.at[me.core, me.x, me.y]
    for d in (2, 1, 3):
        wire.send(part, part, base + 13 + d, me.y_by(d))
    for d in (1, 3, 2):
        wire.recv(o_ref.at[me.core, me.x, wrap(me.y, -d, 4)], base + 13 + d, me.y_by(-d))
    part = o_ref.at[me.core, me.x]
    for d in (2, 1, 3):
        wire.send(part, part, base + 16 + d, me.x_by(d))
    for d in (1, 3, 2):
        wire.recv(o_ref.at[me.core, wrap(me.x, -d, 4)], base + 16 + d, me.x_by(-d))
    wire.send(o_ref.at[me.core], o_ref.at[me.core], base + 20, mate)
    wire.recv(o_ref.at[1 - me.core], base + 20, mate)


def stream_scratch():
    def row(whole):
        first = [buf(2, 4, 2, W, R), buf(4, 2, W, R), buf(2, W, R), buf(2, 2, W, R)]
        return first + ([buf(2, W, R), buf(2, 4, 2, W, R)] if whole else [buf(W, R)])

    col = [buf(16, W, R), buf(2, 4, W // 2, R), buf(2, 4, W, R), buf(3, W, R), buf(W, R), buf(16, W, R)]
    return [buf(16, W, R)] + 2 * (row(True) + col) + row(False)


def whole_kernel(rows, cols, count, center, radius, values, v_ref, new_ref, o_ref, *scratch):
    me = Place()
    send_sem, recv_sem = scratch[-2:]
    image, squares, *sums = scratch[:8]
    mem = scratch[8:-2]
    wire = Wire(send_sem, recv_sem)
    each = len(mem) // STREAMS
    runs = []
    for s in range(STREAMS):
        part = slice(s * W, (s + 1) * W)
        runs.append(stream(me, wire, s * STREAM_SEMS, rows, cols, count, center, radius, values, v_ref.at[part], new_ref.at[part],
                           image.at[part], mem[s * each:(s + 1) * each]))
    deep, zdev = me.deep()
    greet([me.other_core()] + [me.x_by(d) for d in (1, 2, 3)] + [me.y_by(d) for d in (1, 2, 3)] + zdev[1:])
    done, turn = [False] * STREAMS, 0
    while not all(done):
        for s in range(STREAMS):
            if not done[s] and turn >= s * LAG:
                done[s] = next(runs[s], "end") == "end"
        turn += 1
    for i, a in enumerate((new_ref[...], image[...])):
        square = lax.dot_general(a, a, (((1,), (1,)), ((), ())), precision=HIGHEST, preferred_element_type=F32)
        squares[i] = square.reshape(4, 4, 8, VEC)
    sum_all(me, wire, squares, o_ref, *sums, STREAMS * STREAM_SEMS)
    wire.drain()


VMEM = pl.BlockSpec(memory_space=pltpu.VMEM)
SMEM = pl.BlockSpec(memory_space=pltpu.SMEM)


def buf(*dims):
    return pltpu.VMEM(dims, F32)


def out(*dims):
    return jax.ShapeDtypeStruct(dims, F32)


def whole(rows, cols, count, center, radius, values, v):
    n = STREAMS * STREAM_SEMS + SUMS
    scratch = [buf(VEC, R), buf(2, 4, 4, 8, VEC)]
    scratch += [buf(4, 4, 8, VEC), buf(4, 4, 8, VEC), buf(3, 4, 8, VEC), buf(4, 8, VEC), buf(3, 8, VEC), buf(8, 8, VEC)]
    for _ in range(STREAMS):
        scratch += stream_scratch()
    scratch += [pltpu.SemaphoreType.DMA((n,)), pltpu.SemaphoreType.DMA((n,))]
    return pl.pallas_call(
        whole_kernel, out_shape=(out(VEC, R), out(2, 4, 4, 8, VEC)), in_specs=[SMEM] * 5 + [VMEM] * 2, out_specs=(VMEM, VMEM),
        scratch_shapes=scratch, compiler_params=pltpu.CompilerParams(collective_id=0, has_side_effects=True),
    )(rows, cols, count, center, radius, values, v)


def body(start_block, block_values, block_rows, block_cols, block_count, center, radius):
    rows, cols = jnp.clip(block_rows[0], 0, 7), jnp.clip(block_cols[0], 0, 7)
    new, sums = whole(rows, cols, block_count[0], center, radius, block_values[0], start_block.T)
    gram, inner = sums.reshape(2, VEC, VEC)
    lower = jnp.linalg.cholesky(gram)
    solved = jax.scipy.linalg.solve_triangular(lower, jnp.concatenate([new, inner], axis=1), lower=True)
    basis = solved[:, :R].T
    projected = jax.scipy.linalg.solve_triangular(lower, solved[:, R:].T, lower=True)
    return basis, projected


def solution(mesh):
    in_specs = (P(("row", "col"), None), P("row", "col", None, None), P("row", "col"), P("row", "col"), P("row", "col"), P(), P())
    out_specs = (P(("row", "col"), None), P())
    return jax.shard_map(body, mesh=mesh, in_specs=in_specs, out_specs=out_specs, check_vma=False)
```
